128 devices in a mesh: fsdp: 16 (over z_hi, x, core), tensor: 8 (over z_lo, y).
Axes of the slice: x: 4, y: 4, z: 4 (z_hi: 2, z_lo: 2; z = z_hi * 2 + z_lo), core: 2. Of those that a mesh axis runs over, the one named last changes fastest.
Arguments:
- saved_weight: float32 [7168, 8192], P(('fsdp', 'tensor')), may hold values from -6 to 6
- saved_first: float32 [7168, 8192], P(('fsdp', 'tensor')), may hold values from -3 to 3
- saved_second: float32 [7168, 8192], P(('fsdp', 'tensor')), may hold values from 0.1 to 2
- saved_order: int32 [7168], P(('fsdp', 'tensor')), may hold values from 0 to 55, as said below
- mask: int32 [7168, 8192], P('tensor', 'fsdp'), may hold values 0 or 1
- hidden: bfloat16 [4096, 7168], P('fsdp', 'tensor'), may hold values from -6 to 6
- cotangent: bfloat16 [4096, 8192], P('fsdp'), may hold values from -6 to 6
Outputs:
- output: bfloat16 [4096, 8192], P('fsdp', 'tensor')
- hidden_grad: bfloat16 [4096, 7168], P('fsdp', 'tensor')
- new_weight: float32 [7168, 8192], P('tensor', 'fsdp')
- new_first: float32 [7168, 8192], P('tensor', 'fsdp')
- new_second: float32 [7168, 8192], P('tensor', 'fsdp')
The draws below stay inside these ranges and needn't reach their ends.
Inputs may be any that keep to these rules, and one draw needn't show every extreme that they name: `saved_order`: each aligned block of 56 entries holds every number of 0 to 55 once.
All inputs are finite; a program needn't handle non-finite values. No bound on the sum of `mask` on one device may be relied on, other than what follows from the above.
Results may differ from the reference program's by a relative error of at most 0.005.
Values may be sent and summed in bfloat16 or wider, within the bound.
No kernel may reach another device: no remote copies, remote signals or barrier semaphores. Data moves between devices by JAX's collectives and lax.ppermute only.
A program may use at most 128 MiB of HBM per device.

```python
import math
import jax
import jax.numpy as jnp
from jax import lax

D = 8192
R = 7168
STEP = 1000
TOK_DEV = 256
TOKENS = 4096
BAND = 56
N_FSDP = 16


def draw_saved_order(key, part):
    base_rows = jnp.tile(jnp.arange(BAND, dtype=jnp.int32), (R // BAND, 1))
    shuffled = jax.random.permutation(jax.random.fold_in(key, 17), base_rows, axis=1, independent=True)
    return shuffled.reshape(-1).astype(jnp.int32)


def touch_ends(result, rng, smallest, largest):
    place = [jax.random.randint(jax.random.fold_in(rng, axis), (), 0, length) for axis, length in enumerate(result.shape)]
    main_axis = result.shape.index(max(result.shape))
    next_to = place[:main_axis] + [(place[main_axis] + 1) % result.shape[main_axis]] + place[main_axis + 1:]
    return result.at[tuple(place)].set(smallest).at[tuple(next_to)].set(largest)


def raised(values, stream_key, source, target, parts, factor):
    owner, partner = [(jnp.arange(values.shape[position]) // (values.shape[position] // parts)).reshape([-1 if axis == position else 1 for axis in range(values.ndim)]) for position in (source, target)]
    chosen = jax.random.permutation(stream_key, parts)[partner]
    strong = (owner == chosen) | (owner == (partner + parts // 2) % parts)
    return jnp.where(strong, factor * values, values)


def level_of(rng, extent, cuts, low, high):
    level = 1.0
    for axis_at, parts in cuts:
        draws = jax.random.uniform(jax.random.fold_in(jax.random.fold_in(rng, 6), axis_at), (parts,), jnp.float32, low / len(cuts), high / len(cuts))
        level = level * jnp.repeat(jnp.exp(draws), extent[axis_at] // parts).reshape((-1,) + (1,) * (len(extent) - 1 - axis_at))
    return level


def bell_draw(rng, shape, scale, bound, split=(), kind=jnp.bfloat16):
    entries = scale * jax.random.normal(rng, shape, jnp.float32)
    if split:
        entries = entries * level_of(rng, shape, split, -0.22, 0.18)
    return jnp.clip(entries, -bound, bound).astype(kind)


def heavy_noise(stream_key, dims, scale, most, shards, heavy, kind=jnp.bfloat16):
    entries = scale * jax.random.normal(stream_key, dims, jnp.float32)
    if shards:
        entries = entries * level_of(stream_key, dims, shards, -0.22, 0.18)
    return jnp.clip(raised(entries, jax.random.fold_in(stream_key, 3), *heavy), -most, most).astype(kind)


def setup_inputs(seed: int = 0) -> dict:
    key_of = jax.random.split(jax.random.key(seed), 8)
    return {
        "saved_weight": bell_draw(key_of[0], (R, D), 1.0, 6.0, ((0, 128),), jnp.float32),
        "saved_first": bell_draw(key_of[1], (R, D), 0.5, 3.0, ((0, 128),), jnp.float32),
        "saved_second": jnp.clip(jnp.exp(math.log(2.0) - 2.9957323 * jax.random.uniform(key_of[2], (R, D), jnp.float32) ** level_of(key_of[2], (R, D), ((0, 128),), -0.2, 0.2)), 0.1, 2.0),
        "saved_order": draw_saved_order(jax.random.fold_in(key_of[7], 71), 0),
        "mask": touch_ends((jax.random.randint(key_of[4], (R, D), 0, 2) < 1).astype(jnp.int32), jax.random.fold_in(key_of[4], 1), 0, 1),
        "hidden": bell_draw(key_of[5], (TOKENS, R), 1.0, 6.0, ((0, 16), (1, 8))),
        "cotangent": heavy_noise(key_of[6], (TOKENS, D), 1.0, 6.0, ((0, 16),), (0, 1, 16, 2.0)),
    }


beta_first = 0.9
beta_second = 0.999
learn_rate = 0.01
decay_rate = 0.1
epsilon = 1e-08

def reference(saved_weight, saved_first, saved_second, saved_order, mask, hidden, cotangent):
    ordered = saved_order.reshape(-1, BAND)
    offsets = (jnp.arange(ordered.shape[0], dtype=jnp.int32) * BAND)[:, None]
    inverse = (jnp.argsort(ordered, axis=1).astype(jnp.int32) + offsets).reshape(-1)
    weight = jnp.take(saved_weight, inverse, axis=0)
    first = jnp.take(saved_first, inverse, axis=0)
    second = jnp.take(saved_second, inverse, axis=0)
    keep = mask.astype(jnp.float32)
    masked = (weight * keep).astype(jnp.bfloat16)
    scale_alpha = R ** (-0.5)
    output = (scale_alpha * jnp.dot(hidden, masked, preferred_element_type=jnp.float32)).astype(jnp.bfloat16)
    hidden_grad = (scale_alpha * lax.dot_general(cotangent, masked, (((1,), (1,)), ((), ())), preferred_element_type=jnp.float32)).astype(jnp.bfloat16)
    hidden_blocks = hidden.reshape(N_FSDP, TOK_DEV, R)
    cot_blocks = cotangent.reshape(N_FSDP, TOK_DEV, D)

    def accumulate(carry, pair):
        hid_block, cot_block = pair
        partial_sum = lax.dot_general(hid_block, cot_block, (((0,), (0,)), ((), ())), preferred_element_type=jnp.float32)
        rounded = (scale_alpha * partial_sum).astype(jnp.bfloat16)
        return (carry + rounded.astype(jnp.float32), None)
    summed, unused = lax.scan(accumulate, jnp.zeros((R, D), jnp.float32), (hidden_blocks, cot_blocks))
    grad = keep * summed
    new_first = beta_first * first + (1.0 - beta_first) * grad
    new_second = beta_second * second + (1.0 - beta_second) * grad * grad
    corr_first = 1.0 - beta_first ** (STEP + 1)
    corr_second = 1.0 - beta_second ** (STEP + 1)
    update = new_first / corr_first / (jnp.sqrt(new_second / corr_second) + epsilon)
    new_weight = keep * (weight - learn_rate * (update + decay_rate * weight))
    return (output, hidden_grad, new_weight, new_first, new_second)
```

```python
import jax
import jax.numpy as jnp
from jax import lax
from jax.sharding import PartitionSpec as P

R = 7168
STEP = 1000


beta_first = 0.9
beta_second = 0.999
learn_rate = 0.01
decay_rate = 0.1
epsilon = 1e-08


XS = 4
YS = 4
SPREAD = (2, 1, 0, 3)
UNSPREAD = (2, 1, 0, 3)


def fsdp_id(zh, x, core):
    return (zh * XS + x) * 2 + core


def shift_x(value, k):
    pairs = [
        (fsdp_id(zh, x, core), fsdp_id(zh, (x + k) % XS, core))
        for zh in range(2)
        for x in range(XS)
        for core in range(2)
    ]
    return lax.ppermute(value, "fsdp", pairs)


def swap_zh(value):
    return lax.ppermute(value, "fsdp", [(i, i ^ 8) for i in range(16)])


def swap_core(value):
    return lax.ppermute(value, "fsdp", [(i, i ^ 1) for i in range(16)])


def shift_y(value, k):
    pairs = [(zl * YS + y, zl * YS + (y + k) % YS) for zl in range(2) for y in range(YS)]
    return lax.ppermute(value, "tensor", pairs)


def swap_zl(value):
    return lax.ppermute(value, "tensor", [(i, i ^ 4) for i in range(8)])


def place_output(value):
    pairs = []
    for f in range(16):
        zh, x, core = f // 8, (f // 2) % 4, f % 2
        for t in range(8):
            zl, y = t // 4, t % 4
            there = fsdp_id(zh, (x + SPREAD[(y - x) % 4]) % XS, core)
            pairs.append((f * 8 + t, there * 8 + zl * YS + x))
    return lax.ppermute(value, ("fsdp", "tensor"), pairs)


def body(saved_weight, saved_first, saved_second, saved_order, mask, hidden, cotangent):
    f32, bf16 = jnp.float32, jnp.bfloat16
    band = saved_order.shape[0]
    toks, rows = hidden.shape
    cols = mask.shape[1]
    f = lax.axis_index("fsdp")
    t = lax.axis_index("tensor")
    zh, x, core = f // 8, (f // 2) % 4, f % 2
    zl, y = t // 4, t % 4
    alpha = R ** (-0.5)

    pick = (saved_order[None, :] == jnp.arange(band, dtype=jnp.int32)[:, None]).astype(bf16)

    def arranged(saved):
        moved = jnp.dot(pick, saved.astype(bf16), preferred_element_type=f32).astype(bf16)
        return moved.reshape(band, 16, cols).transpose(1, 0, 2)

    def relayed(blocks):
        n = blocks.shape[1]
        got = lax.all_to_all(blocks, "fsdp", split_axis=0, concat_axis=0, tiled=True)
        got = lax.all_to_all(got, "tensor", split_axis=0, concat_axis=0, tiled=True)
        return got.reshape(8, 2, n, cols).transpose(1, 0, 2, 3).reshape(16, n, cols)

    weight = relayed(arranged(saved_weight)).reshape(rows, cols)
    masked = weight * mask.astype(bf16)

    hidden_all = jnp.concatenate([hidden] + [shift_x(hidden, k) for k in (1, 2, 3)], axis=0)

    def cot_for(k):
        there = (x + k) % XS
        parts = [
            lax.dynamic_slice_in_dim(
                cotangent, fsdp_id(zh ^ zr, there, core ^ cr) * cols, cols, axis=1
            )
            for zr in (0, 1)
            for cr in (0, 1)
        ]
        return jnp.concatenate(parts, axis=1)

    cot_all = jnp.concatenate([cot_for(0)] + [shift_x(cot_for(k), k) for k in (1, 2, 3)], axis=0)

    masked_zh = swap_zh(masked)
    columns = jnp.concatenate(
        [masked, swap_core(masked), masked_zh, swap_core(masked_zh)], axis=1
    )

    partial_out = (
        alpha * jnp.dot(hidden_all, columns, preferred_element_type=f32)
    ).astype(bf16).reshape(XS, toks, 4 * cols)

    def chunk_of(yy):
        e = (yy - x) % 4
        there = jnp.where(e == 0, SPREAD[0], jnp.where(e == 2, SPREAD[2], e))
        return lax.dynamic_index_in_dim(partial_out, (-there) % 4, axis=0, keepdims=False)

    total = chunk_of(y).astype(f32)
    for k in (1, 2, 3):
        total = total + shift_y(chunk_of((y + k) % YS), k).astype(f32)
    total = total.reshape(toks, 2, 2, cols)
    mine = lax.dynamic_index_in_dim(total, zh ^ zl, axis=1, keepdims=False)
    other = lax.dynamic_index_in_dim(total, 1 - (zh ^ zl), axis=1, keepdims=False)
    reduced = (mine + swap_zl(other.astype(bf16)).astype(f32)).astype(bf16)
    reduced = jnp.where(core == 0, reduced, reduced[:, ::-1]).reshape(toks, 2 * cols)
    output = place_output(reduced)

    back = (
        alpha
        * lax.dot_general(cot_all, columns, (((1,), (1,)), ((), ())), preferred_element_type=f32)
    ).reshape(XS, toks, rows)
    hidden_grad = back[0]
    for k in (1, 2, 3):
        hidden_grad = hidden_grad + shift_x(back[k].astype(bf16), -k).astype(f32)
    hidden_grad = hidden_grad.astype(bf16)

    product = (
        alpha
        * lax.dot_general(hidden_all, cot_all, (((0,), (0,)), ((), ())), preferred_element_type=f32)
    ).astype(bf16).reshape(rows, 2, 2, cols)
    from_core = swap_core(product[:, :, 1])
    near = product[:, 0, 0].astype(f32) + from_core[:, 0].astype(f32)
    far = (product[:, 1, 0].astype(f32) + from_core[:, 1].astype(f32)).astype(bf16)
    summed = near + swap_zh(far).astype(f32)

    moments = relayed(jnp.concatenate([arranged(saved_first), arranged(saved_second)], axis=1))
    first = moments[:, :band].reshape(rows, cols).astype(f32)
    second = moments[:, band:].reshape(rows, cols).astype(f32)
    weight = weight.astype(f32)

    keep = mask.astype(f32)
    grad = keep * summed
    new_first = beta_first * first + (1.0 - beta_first) * grad
    new_second = beta_second * second + (1.0 - beta_second) * grad * grad
    corr_first = 1.0 - beta_first ** (STEP + 1)
    corr_second = 1.0 - beta_second ** (STEP + 1)
    update = new_first / corr_first / (jnp.sqrt(new_second / corr_second) + epsilon)
    new_weight = keep * (weight - learn_rate * (update + decay_rate * weight))
    return (output, hidden_grad, new_weight, new_first, new_second)


def solution(mesh):
    return jax.shard_map(
        body,
        mesh=mesh,
        in_specs=(
            P(("fsdp", "tensor"), None),
            P(("fsdp", "tensor"), None),
            P(("fsdp", "tensor"), None),
            P(("fsdp", "tensor")),
            P("tensor", "fsdp"),
            P("fsdp", "tensor"),
            P("fsdp", None),
        ),
        out_specs=(
            P("fsdp", "tensor"),
            P("fsdp", "tensor"),
            P("tensor", "fsdp"),
            P("tensor", "fsdp"),
            P("tensor", "fsdp"),
        ),
        check_vma=False,
    )
```

```python
import jax
import jax.numpy as jnp
from jax import lax
from jax.sharding import PartitionSpec as P


R = 7168
STEP = 1000


beta_first = 0.9
beta_second = 0.999
learn_rate = 0.01
decay_rate = 0.1
epsilon = 1e-08


XS = 4
YS = 4
SPREAD = (2, 1, 0, 3)


def fsdp_id(zh, x, core):
    return (zh * XS + x) * 2 + core


def shift_x(value, k):
    pairs = [
        (fsdp_id(zh, x, core), fsdp_id(zh, (x + k) % XS, core))
        for zh in range(2)
        for x in range(XS)
        for core in range(2)
    ]
    return lax.ppermute(value, "fsdp", pairs)


def swap_zh(value):
    return lax.ppermute(value, "fsdp", [(i, i ^ 8) for i in range(16)])


def swap_core(value):
    return lax.ppermute(value, "fsdp", [(i, i ^ 1) for i in range(16)])


def shift_y(value, k):
    pairs = [(zl * YS + y, zl * YS + (y + k) % YS) for zl in range(2) for y in range(YS)]
    return lax.ppermute(value, "tensor", pairs)


def swap_zl_half(value, near):
    pairs = []
    for f in range(16):
        keeper = f // 8 if near else 1 - f // 8
        for y in range(YS):
            pairs.append((f * 8 + (1 - keeper) * YS + y, f * 8 + keeper * YS + y))
    return lax.ppermute(value, ("fsdp", "tensor"), pairs)


def place_output(value, near):
    pairs = []
    for f in range(16):
        zh, x, core = f // 8, (f // 2) % 4, f % 2
        zl = zh if near else 1 - zh
        for y in range(YS):
            there = fsdp_id(zh, (x + SPREAD[(y - x) % 4]) % XS, core)
            pairs.append((f * 8 + zl * YS + y, there * 8 + zl * YS + x))
    return lax.ppermute(value, ("fsdp", "tensor"), pairs)


def stacked(pieces):
    n = pieces[0].shape[0]
    whole = jnp.zeros((n * len(pieces),) + pieces[0].shape[1:], pieces[0].dtype)
    for k, piece in enumerate(pieces):
        whole = lax.dynamic_update_slice_in_dim(whole, piece, k * n, axis=0)
    return whole


def body(saved_weight, saved_first, saved_second, saved_order, mask, hidden, cotangent):
    f32, bf16 = jnp.float32, jnp.bfloat16
    band = saved_order.shape[0]
    toks, rows = hidden.shape
    cols = mask.shape[1]
    f = lax.axis_index("fsdp")
    t = lax.axis_index("tensor")
    zh, x, core = f >> 3, (f >> 1) & 3, f & 1
    zl, y = t >> 2, t & 3
    alpha = R ** (-0.5)

    pick = (saved_order[None, :] == jnp.arange(band, dtype=jnp.int32)[:, None]).astype(bf16)

    def arranged(saved):
        moved = jnp.dot(pick, saved.astype(bf16), preferred_element_type=f32).astype(bf16)
        return moved.reshape(band, 16, cols).transpose(1, 0, 2)

    def to_columns(blocks):
        return lax.all_to_all(blocks, "fsdp", split_axis=0, concat_axis=0, tiled=True)

    def to_rows(blocks):
        n = blocks.shape[1]
        got = lax.all_to_all(blocks, "tensor", split_axis=0, concat_axis=0, tiled=True)
        return got.reshape(8, 2, n, cols).transpose(1, 0, 2, 3).reshape(16, n, cols)

    weight_columns = to_columns(arranged(saved_weight))
    weight = to_rows(weight_columns).reshape(rows, cols)
    masked = weight * mask.astype(bf16)

    pieces = [hidden]
    for k in (1, 2, 3):
        pieces.append(shift_x(hidden, k))
    hidden_all = stacked(pieces)

    def cot_for(k):
        there = (x + k) & 3
        parts = [
            lax.dynamic_slice_in_dim(
                cotangent, fsdp_id(zh ^ zr, there, core ^ cr) * cols, cols, axis=1
            )
            for cr in (0, 1)
            for zr in (0, 1)
        ]
        return jnp.concatenate(parts, axis=1)

    pieces = [cot_for(0)]
    for k in (1, 2, 3):
        pieces.append(shift_x(cot_for(k), k))
    cot_pieces = pieces

    masked_core = swap_core(masked)
    masked_zh = swap_zh(masked)
    masked_far = swap_core(masked_zh)

    def output_half(own, other, near):
        parts = []
        for block in (own, other):
            product = alpha * jnp.dot(hidden_all, block, preferred_element_type=f32)
            parts.append(product.astype(bf16).reshape(XS, toks, cols))

        def chunk_of(yy):
            e = (yy - x) & 3
            there = jnp.where(e == 0, SPREAD[0], jnp.where(e == 2, SPREAD[2], e))
            k = (-there) & 3
            return jnp.concatenate(
                [lax.dynamic_index_in_dim(p, k, axis=0, keepdims=False) for p in parts], axis=1
            )

        got = []
        for k in (1, 2, 3):
            got.append(shift_y(chunk_of((y + k) & 3), k))
        own_chunk = chunk_of(y)
        total = own_chunk.astype(f32)
        for piece in got:
            total = total + piece.astype(f32)
        sent = total.astype(bf16)
        got = swap_zl_half(sent, near)
        total = (total + got.astype(f32)).astype(bf16)
        total = jnp.where(
            core == 0, total, jnp.concatenate([total[:, cols:], total[:, :cols]], axis=1)
        )
        return place_output(total, near)

    out_near = output_half(masked, masked_core, True)
    out_far = output_half(masked_zh, masked_far, False)
    output = jnp.where(zl == zh, out_near, out_far)

    columns = jnp.concatenate([masked, masked_zh, masked_core, masked_far], axis=1)
    cot_all = stacked(cot_pieces)
    back = (
        alpha
        * lax.dot_general(cot_all, columns, (((1,), (1,)), ((), ())), preferred_element_type=f32)
    ).astype(bf16).reshape(XS, toks, rows)
    got = []
    for k in (1, 2, 3):
        got.append(shift_x(back[k], -k))
    hidden_grad = back[0].astype(f32)
    for piece in got:
        hidden_grad = hidden_grad + piece.astype(f32)
    hidden_grad = hidden_grad.astype(bf16)

    def product(block):
        return (
            alpha
            * lax.dot_general(
                hidden_all, block, (((0,), (0,)), ((), ())), preferred_element_type=f32
            )
        ).astype(bf16)

    away = product(cot_all[:, 2 * cols :])
    stay = product(cot_all[:, : 2 * cols])
    from_core = swap_core(away)
    far = (stay[:, cols:].astype(f32) + from_core[:, cols:].astype(f32)).astype(bf16)
    from_zh = swap_zh(far)
    summed = stay[:, :cols].astype(f32) + from_core[:, :cols].astype(f32) + from_zh.astype(f32)

    moment_blocks = jnp.concatenate(
        [arranged(saved_first), arranged(saved_second)], axis=1
    )
    moments = to_columns(moment_blocks)
    moments = to_rows(moments)
    first = moments[:, :band].reshape(rows, cols).astype(f32)
    second = moments[:, band:].reshape(rows, cols).astype(f32)
    weight = weight.astype(f32)

    keep = mask.astype(f32)
    grad = keep * summed
    new_first = beta_first * first + (1.0 - beta_first) * grad
    new_second = beta_second * second + (1.0 - beta_second) * grad * grad
    corr_first = 1.0 - beta_first ** (STEP + 1)
    corr_second = 1.0 - beta_second ** (STEP + 1)
    update = new_first / corr_first / (jnp.sqrt(new_second / corr_second) + epsilon)
    new_weight = keep * (weight - learn_rate * (update + decay_rate * weight))
    return (output, hidden_grad, new_weight, new_first, new_second)


def solution(mesh):
    return jax.shard_map(
        body,
        mesh=mesh,
        in_specs=(
            P(("fsdp", "tensor"), None),
            P(("fsdp", "tensor"), None),
            P(("fsdp", "tensor"), None),
            P(("fsdp", "tensor")),
            P("tensor", "fsdp"),
            P("fsdp", "tensor"),
            P("fsdp", None),
        ),
        out_specs=(
            P("fsdp", "tensor"),
            P("fsdp", "tensor"),
            P("tensor", "fsdp"),
            P("tensor", "fsdp"),
            P("tensor", "fsdp"),
        ),
        check_vma=False,
    )
```

```python
import jax
import jax.numpy as jnp
from jax import lax
from jax.experimental import pallas as pl
from jax.experimental.pallas import tpu as pltpu
from jax.sharding import PartitionSpec as P


R = 7168
STEP = 1000


beta_first = 0.9
beta_second = 0.999
learn_rate = 0.01
decay_rate = 0.1
epsilon = 1e-08


XS = 4
YS = 4
TILE = 512
SPREAD = (2, 1, 0, 3)


def fsdp_id(zh, x, core):
    return (zh * XS + x) * 2 + core


def shift_x(value, k):
    pairs = [
        (fsdp_id(zh, x, core), fsdp_id(zh, (x + k) % XS, core))
        for zh in range(2)
        for x in range(XS)
        for core in range(2)
    ]
    return lax.ppermute(value, "fsdp", pairs)


def swap_zh(value):
    return lax.ppermute(value, "fsdp", [(i, i ^ 8) for i in range(16)])


def swap_core(value):
    return lax.ppermute(value, "fsdp", [(i, i ^ 1) for i in range(16)])


def shift_y(value, k):
    pairs = [(zl * YS + y, zl * YS + (y + k) % YS) for zl in range(2) for y in range(YS)]
    return lax.ppermute(value, "tensor", pairs)


def swap_zl_half(value, near):
    pairs = []
    for f in range(16):
        keeper = f // 8 if near else 1 - f // 8
        for y in range(YS):
            pairs.append((f * 8 + (1 - keeper) * YS + y, f * 8 + keeper * YS + y))
    return lax.ppermute(value, ("fsdp", "tensor"), pairs)


def place_output(value, near):
    pairs = []
    for f in range(16):
        zh, x, core = f // 8, (f // 2) % 4, f % 2
        zl = zh if near else 1 - zh
        for y in range(YS):
            there = fsdp_id(zh, (x + SPREAD[(y - x) % 4]) % XS, core)
            pairs.append((f * 8 + zl * YS + y, there * 8 + zl * YS + x))
    return lax.ppermute(value, ("fsdp", "tensor"), pairs)


VMEM = pl.BlockSpec(memory_space=pltpu.VMEM)
SMEM = pl.BlockSpec(memory_space=pltpu.SMEM)


def forward_kernel(order, h0, h1, h2, h3, own, other, o0, o1, o2, o3, h):
    alpha = R ** (-0.5)
    cols = own.shape[1]
    for k, piece in enumerate((h0, h1, h2, h3)):
        h[k] = piece[...]
    for j, out in enumerate((o0, o1, o2, o3)):
        block_of = h[order[j]]
        for i, block in enumerate((own, other)):
            product = jnp.dot(block_of, block[...], preferred_element_type=jnp.float32)
            out[:, i * cols : (i + 1) * cols] = (alpha * product).astype(jnp.bfloat16)


def forward(order, pieces, own, other):
    (toks, depth), width = pieces[0].shape, 2 * own.shape[1]
    return pl.pallas_call(
        forward_kernel,
        in_specs=[SMEM] + [VMEM] * (XS + 2),
        out_specs=[VMEM] * XS,
        out_shape=[jax.ShapeDtypeStruct((toks, width), jnp.bfloat16)] * XS,
        scratch_shapes=[pltpu.VMEM((XS, toks, depth), jnp.bfloat16)],
        cost_estimate=pl.CostEstimate(
            flops=2 * XS * toks * depth * width,
            bytes_accessed=2 * (XS * toks * depth + depth * width + XS * toks * width),
            transcendentals=0,
        ),
        name="forward",
    )(order, *pieces, own, other)


def turned_product(h_turned, c_refs, lo, hi):
    columns = jnp.concatenate([c[:, lo:hi] for c in c_refs], axis=0)
    product = jnp.dot(h_turned[...], columns, preferred_element_type=jnp.float32)
    return (R ** (-0.5) * product).astype(jnp.bfloat16)


def away_kernel(h0, h1, h2, h3, c0, c1, c2, c3, out, h_turned):
    toks = h0.shape[0]
    for k, piece in enumerate((h0, h1, h2, h3)):
        h_turned[:, k * toks : (k + 1) * toks] = piece[...].T
    half = out.shape[1]
    for lo in range(0, half, TILE):
        out[:, lo : lo + TILE] = turned_product(
            h_turned, (c0, c1, c2, c3), half + lo, half + lo + TILE
        )


def stay_kernel(h_turned, c0, c1, c2, c3, out):
    for lo in range(0, out.shape[1], TILE):
        out[:, lo : lo + TILE] = turned_product(h_turned, (c0, c1, c2, c3), lo, lo + TILE)


def gradient_cost(pieces, cots):
    toks, depth = pieces[0].shape
    half = cots[0].shape[1] // 2
    return pl.CostEstimate(
        flops=2 * XS * toks * depth * half,
        bytes_accessed=2 * (XS * toks * (depth + half) + depth * half),
        transcendentals=0,
    )


def gradient_away(pieces, cots):
    toks, depth = pieces[0].shape
    half = cots[0].shape[1] // 2
    return pl.pallas_call(
        away_kernel,
        in_specs=[VMEM] * (2 * XS),
        out_specs=[VMEM] * 2,
        out_shape=[
            jax.ShapeDtypeStruct((depth, half), jnp.bfloat16),
            jax.ShapeDtypeStruct((depth, XS * toks), jnp.bfloat16),
        ],
        cost_estimate=gradient_cost(pieces, cots),
        name="away",
    )(*pieces, *cots)


def gradient_stay(turned, pieces, cots):
    depth = pieces[0].shape[1]
    half = cots[0].shape[1] // 2
    return pl.pallas_call(
        stay_kernel,
        in_specs=[VMEM] * (1 + XS),
        out_specs=VMEM,
        out_shape=jax.ShapeDtypeStruct((depth, half), jnp.bfloat16),
        cost_estimate=gradient_cost(pieces, cots),
        name="stay",
    )(turned, *cots)


def backward_kernel(c0, c1, c2, c3, w0, w1, w2, w3, o0, o1, o2, o3):
    alpha = R ** (-0.5)
    cols = w0.shape[1]
    for c, out in ((c0, o0), (c1, o1), (c2, o2), (c3, o3)):
        total = None
        for i, w in enumerate((w0, w1, w2, w3)):
            part = lax.dot_general(
                c[:, i * cols : (i + 1) * cols],
                w[...],
                (((1,), (1,)), ((), ())),
                preferred_element_type=jnp.float32,
            )
            total = part if total is None else total + part
        out[...] = (alpha * total).astype(jnp.bfloat16)


def backward(pieces, blocks):
    toks, rows = pieces[0].shape[0], blocks[0].shape[0]
    return pl.pallas_call(
        backward_kernel,
        in_specs=[VMEM] * 8,
        out_specs=[VMEM] * XS,
        out_shape=[jax.ShapeDtypeStruct((toks, rows), jnp.bfloat16)] * XS,
        cost_estimate=pl.CostEstimate(
            flops=8 * pieces[0].size * rows,
            bytes_accessed=8 * (pieces[0].size + blocks[0].size + toks * rows),
            transcendentals=0,
        ),
        name="backward",
    )(*pieces, *blocks)


def body(saved_weight, saved_first, saved_second, saved_order, mask, hidden, cotangent):
    f32, bf16 = jnp.float32, jnp.bfloat16
    band = saved_order.shape[0]
    _, rows = hidden.shape
    cols = mask.shape[1]
    f = lax.axis_index("fsdp")
    t = lax.axis_index("tensor")
    zh, x, core = f >> 3, (f >> 1) & 3, f & 1
    zl, y = t >> 2, t & 3

    pick = (saved_order[None, :] == jnp.arange(band, dtype=jnp.int32)[:, None]).astype(bf16)

    def arranged(saved):
        moved = jnp.dot(pick, saved.astype(bf16), preferred_element_type=f32).astype(bf16)
        return moved.reshape(band, 16, cols).transpose(1, 0, 2)

    def to_columns(blocks):
        return lax.all_to_all(blocks, "fsdp", split_axis=0, concat_axis=0, tiled=True)

    def to_rows(blocks):
        n = blocks.shape[1]
        got = lax.all_to_all(blocks, "tensor", split_axis=0, concat_axis=0, tiled=True)
        return got.reshape(8, 2, n, cols).transpose(1, 0, 2, 3).reshape(16, n, cols)

    weight_columns = to_columns(arranged(saved_weight))
    weight = to_rows(weight_columns).reshape(rows, cols)
    masked = weight * mask.astype(bf16)

    pieces = [hidden]
    for k in (1, 2, 3):
        pieces.append(shift_x(hidden, k))
    hidden_pieces = pieces

    def cot_for(k):
        there = (x + k) & 3
        parts = [
            lax.dynamic_slice_in_dim(
                cotangent, fsdp_id(zh ^ zr, there, core ^ cr) * cols, cols, axis=1
            )
            for cr in (0, 1)
            for zr in (0, 1)
        ]
        return jnp.concatenate(parts, axis=1)

    pieces = [cot_for(0)]
    for k in (1, 2, 3):
        pieces.append(shift_x(cot_for(k), k))
    cot_pieces = pieces

    masked_core = swap_core(masked)
    masked_zh = swap_zh(masked)
    masked_far = swap_core(masked_zh)

    def token_block_at(yy):
        e = (yy - x) & 3
        there = jnp.where(e == 0, SPREAD[0], jnp.where(e == 2, SPREAD[2], e))
        return (-there) & 3

    order = jnp.stack([token_block_at((y + k) & 3) for k in range(YS)]).astype(jnp.int32)

    def output_half(own, other, near):
        chunks = forward(order, hidden_pieces, own, other)
        own_chunk = chunks[0]
        got = []
        for k in (1, 2, 3):
            got.append(shift_y(chunks[k], k))
        total = own_chunk.astype(f32)
        for piece in got:
            total = total + piece.astype(f32)
        sent = total.astype(bf16)
        got = swap_zl_half(sent, near)
        total = (total + got.astype(f32)).astype(bf16)
        total = jnp.where(
            core == 0, total, jnp.concatenate([total[:, cols:], total[:, :cols]], axis=1)
        )
        return place_output(total, near)

    out_near = output_half(masked, masked_core, True)
    out_far = output_half(masked_zh, masked_far, False)
    output = jnp.where(zl == zh, out_near, out_far)

    back = backward(cot_pieces, [masked, masked_zh, masked_core, masked_far])
    got = []
    for k in (1, 2, 3):
        got.append(shift_x(back[k], -k))
    hidden_grad = back[0].astype(f32)
    for piece in got:
        hidden_grad = hidden_grad + piece.astype(f32)
    hidden_grad = hidden_grad.astype(bf16)

    away, turned = gradient_away(hidden_pieces, cot_pieces)
    stay = gradient_stay(turned, hidden_pieces, cot_pieces)
    from_core = swap_core(away)
    far = (stay[:, cols:].astype(f32) + from_core[:, cols:].astype(f32)).astype(bf16)
    from_zh = swap_zh(far)
    summed = stay[:, :cols].astype(f32) + from_core[:, :cols].astype(f32) + from_zh.astype(f32)

    moment_blocks = jnp.concatenate(
        [arranged(saved_first), arranged(saved_second)], axis=1
    )
    moments = to_columns(moment_blocks)
    moments = to_rows(moments)
    first = moments[:, :band].reshape(rows, cols).astype(f32)
    second = moments[:, band:].reshape(rows, cols).astype(f32)
    weight = weight.astype(f32)

    keep = mask.astype(f32)
    grad = keep * summed
    new_first = beta_first * first + (1.0 - beta_first) * grad
    new_second = beta_second * second + (1.0 - beta_second) * grad * grad
    corr_first = 1.0 - beta_first ** (STEP + 1)
    corr_second = 1.0 - beta_second ** (STEP + 1)
    update = new_first / corr_first / (jnp.sqrt(new_second / corr_second) + epsilon)
    new_weight = keep * (weight - learn_rate * (update + decay_rate * weight))
    return (output, hidden_grad, new_weight, new_first, new_second)


def solution(mesh):
    return jax.shard_map(
        body,
        mesh=mesh,
        in_specs=(
            P(("fsdp", "tensor"), None),
            P(("fsdp", "tensor"), None),
            P(("fsdp", "tensor"), None),
            P(("fsdp", "tensor")),
            P("tensor", "fsdp"),
            P("fsdp", "tensor"),
            P("fsdp", None),
        ),
        out_specs=(
            P("fsdp", "tensor"),
            P("fsdp", "tensor"),
            P("tensor", "fsdp"),
            P("tensor", "fsdp"),
            P("tensor", "fsdp"),
        ),
        check_vma=False,
    )
```

```python
import jax
import jax.numpy as jnp
from jax import lax
from jax.experimental import pallas as pl
from jax.experimental.pallas import tpu as pltpu
from jax.sharding import PartitionSpec as P


R = 7168
STEP = 1000


beta_first = 0.9
beta_second = 0.999
learn_rate = 0.01
decay_rate = 0.1
epsilon = 1e-08


XS = 4
YS = 4
TILE = 512
SPREAD = (2, 1, 0, 3)


def fsdp_id(zh, x, core):
    return (zh * XS + x) * 2 + core


def shift_x(value, k):
    pairs = [
        (fsdp_id(zh, x, core), fsdp_id(zh, (x + k) % XS, core))
        for zh in range(2)
        for x in range(XS)
        for core in range(2)
    ]
    return lax.ppermute(value, "fsdp", pairs)


def swap_zh(value):
    return lax.ppermute(value, "fsdp", [(i, i ^ 8) for i in range(16)])


def swap_core(value):
    return lax.ppermute(value, "fsdp", [(i, i ^ 1) for i in range(16)])


def shift_y(value, k):
    pairs = [(zl * YS + y, zl * YS + (y + k) % YS) for zl in range(2) for y in range(YS)]
    return lax.ppermute(value, "tensor", pairs)


def swap_zl_half(value, near):
    pairs = []
    for f in range(16):
        keeper = f // 8 if near else 1 - f // 8
        for y in range(YS):
            pairs.append((f * 8 + (1 - keeper) * YS + y, f * 8 + keeper * YS + y))
    return lax.ppermute(value, ("fsdp", "tensor"), pairs)


def place_output(value, near):
    pairs = []
    for f in range(16):
        zh, x, core = f // 8, (f // 2) % 4, f % 2
        zl = zh if near else 1 - zh
        for y in range(YS):
            there = fsdp_id(zh, (x + SPREAD[(y - x) % 4]) % XS, core)
            pairs.append((f * 8 + zl * YS + y, there * 8 + zl * YS + x))
    return lax.ppermute(value, ("fsdp", "tensor"), pairs)


VMEM = pl.BlockSpec(memory_space=pltpu.VMEM)
SMEM = pl.BlockSpec(memory_space=pltpu.SMEM)


def forward_kernel(order, h0, h1, h2, h3, own, other, o0, o1, o2, o3, h):
    alpha = R ** (-0.5)
    cols = own.shape[1]
    for k, piece in enumerate((h0, h1, h2, h3)):
        h[k] = piece[...]
    for j, out in enumerate((o0, o1, o2, o3)):
        block_of = h[order[j]]
        for i, block in enumerate((own, other)):
            product = jnp.dot(block_of, block[...], preferred_element_type=jnp.float32)
            out[:, i * cols : (i + 1) * cols] = (alpha * product).astype(jnp.bfloat16)


def forward(order, pieces, own, other):
    (toks, depth), width = pieces[0].shape, 2 * own.shape[1]
    return pl.pallas_call(
        forward_kernel,
        in_specs=[SMEM] + [VMEM] * (XS + 2),
        out_specs=[VMEM] * XS,
        out_shape=[jax.ShapeDtypeStruct((toks, width), jnp.bfloat16)] * XS,
        scratch_shapes=[pltpu.VMEM((XS, toks, depth), jnp.bfloat16)],
        cost_estimate=pl.CostEstimate(
            flops=2 * XS * toks * depth * width,
            bytes_accessed=2 * (XS * toks * depth + depth * width + XS * toks * width),
            transcendentals=0,
        ),
        name="forward",
    )(order, *pieces, own, other)


def joined_kernel(at, q0, q1, q2, q3, out):
    part = q0.shape[0]
    for k, piece in enumerate((q0, q1, q2, q3)):
        out[pl.ds(pl.multiple_of(at[k] * part, part), part), :] = piece[...]


def joined(at, pieces):
    part, width = pieces[0].shape
    return pl.pallas_call(
        joined_kernel,
        in_specs=[SMEM] + [VMEM] * YS,
        out_specs=VMEM,
        out_shape=jax.ShapeDtypeStruct((YS * part, width), pieces[0].dtype),
        cost_estimate=pl.CostEstimate(
            flops=0, bytes_accessed=4 * YS * part * width, transcendentals=0
        ),
        name="joined",
    )(at, *pieces)


def turned_product(h_turned, c_refs, lo, hi):
    columns = jnp.concatenate([c[:, lo:hi] for c in c_refs], axis=0)
    product = jnp.dot(h_turned[...], columns, preferred_element_type=jnp.float32)
    return (R ** (-0.5) * product).astype(jnp.bfloat16)


def away_kernel(h0, h1, h2, h3, c0, c1, c2, c3, out, h_turned):
    toks = h0.shape[0]
    for k, piece in enumerate((h0, h1, h2, h3)):
        h_turned[:, k * toks : (k + 1) * toks] = piece[...].T
    half = out.shape[1]
    for lo in range(0, half, TILE):
        out[:, lo : lo + TILE] = turned_product(
            h_turned, (c0, c1, c2, c3), half + lo, half + lo + TILE
        )


def stay_kernel(h_turned, c0, c1, c2, c3, out):
    for lo in range(0, out.shape[1], TILE):
        out[:, lo : lo + TILE] = turned_product(h_turned, (c0, c1, c2, c3), lo, lo + TILE)


def gradient_cost(pieces, cots):
    toks, depth = pieces[0].shape
    half = cots[0].shape[1] // 2
    return pl.CostEstimate(
        flops=2 * XS * toks * depth * half,
        bytes_accessed=2 * (XS * toks * (depth + half) + depth * half),
        transcendentals=0,
    )


def gradient_away(pieces, cots):
    toks, depth = pieces[0].shape
    half = cots[0].shape[1] // 2
    return pl.pallas_call(
        away_kernel,
        in_specs=[VMEM] * (2 * XS),
        out_specs=[VMEM] * 2,
        out_shape=[
            jax.ShapeDtypeStruct((depth, half), jnp.bfloat16),
            jax.ShapeDtypeStruct((depth, XS * toks), jnp.bfloat16),
        ],
        cost_estimate=gradient_cost(pieces, cots),
        name="away",
    )(*pieces, *cots)


def gradient_stay(turned, pieces, cots):
    depth = pieces[0].shape[1]
    half = cots[0].shape[1] // 2
    return pl.pallas_call(
        stay_kernel,
        in_specs=[VMEM] * (1 + XS),
        out_specs=VMEM,
        out_shape=jax.ShapeDtypeStruct((depth, half), jnp.bfloat16),
        cost_estimate=gradient_cost(pieces, cots),
        name="stay",
    )(turned, *cots)


def backward_kernel(c0, c1, c2, c3, w0, w1, w2, w3, o0, o1, o2, o3):
    alpha = R ** (-0.5)
    cols = w0.shape[1]
    for c, out in ((c0, o0), (c1, o1), (c2, o2), (c3, o3)):
        total = None
        for i, w in enumerate((w0, w1, w2, w3)):
            part = lax.dot_general(
                c[:, i * cols : (i + 1) * cols],
                w[...],
                (((1,), (1,)), ((), ())),
                preferred_element_type=jnp.float32,
            )
            total = part if total is None else total + part
        out[...] = (alpha * total).astype(jnp.bfloat16)


def backward(pieces, blocks):
    toks, rows = pieces[0].shape[0], blocks[0].shape[0]
    return pl.pallas_call(
        backward_kernel,
        in_specs=[VMEM] * 8,
        out_specs=[VMEM] * XS,
        out_shape=[jax.ShapeDtypeStruct((toks, rows), jnp.bfloat16)] * XS,
        cost_estimate=pl.CostEstimate(
            flops=8 * pieces[0].size * rows,
            bytes_accessed=8 * (pieces[0].size + blocks[0].size + toks * rows),
            transcendentals=0,
        ),
        name="backward",
    )(*pieces, *blocks)


def body(saved_weight, saved_first, saved_second, saved_order, mask, hidden, cotangent):
    f32, bf16 = jnp.float32, jnp.bfloat16
    band = saved_order.shape[0]
    toks, rows = hidden.shape
    cols = mask.shape[1]
    f = lax.axis_index("fsdp")
    t = lax.axis_index("tensor")
    zh, x, core = f >> 3, (f >> 1) & 3, f & 1
    zl, y = t >> 2, t & 3

    pick = (saved_order[None, :] == jnp.arange(band, dtype=jnp.int32)[:, None]).astype(bf16)

    def arranged(saved):
        moved = jnp.dot(pick, saved.astype(bf16), preferred_element_type=f32).astype(bf16)
        return moved.reshape(band, 16, cols).transpose(1, 0, 2)

    def to_columns(blocks):
        return lax.all_to_all(blocks, "fsdp", split_axis=0, concat_axis=0, tiled=True)

    def to_rows(blocks):
        n = blocks.shape[1]
        got = lax.all_to_all(blocks, "tensor", split_axis=0, concat_axis=0, tiled=True)
        return got.reshape(8, 2, n, cols).transpose(1, 0, 2, 3).reshape(16, n, cols)

    weight_columns = to_columns(arranged(saved_weight))
    weight = to_rows(weight_columns).reshape(rows, cols)
    masked = weight * mask.astype(bf16)

    pieces = [hidden]
    for k in (1, 2, 3):
        pieces.append(shift_x(hidden, k))
    hidden_pieces = pieces

    def cot_for(k, first_row, n):
        there = (x + k) & 3
        parts = [
            lax.dynamic_slice(
                cotangent, (first_row, fsdp_id(zh ^ zr, there, core ^ cr) * cols), (n, cols)
            )
            for cr in (0, 1)
            for zr in (0, 1)
        ]
        return jnp.concatenate(parts, axis=1)

    part = toks // YS
    quarter = shift_x(cot_for(2, y * part, part), 2)
    pieces = [cot_for(0, 0, toks)]
    pieces.append(shift_x(cot_for(1, 0, toks), 1))
    last = shift_x(cot_for(3, 0, toks), 3)
    quarters = [quarter]
    for k in (1, 2, 3):
        quarters.append(shift_y(quarter, k))
    at = jnp.stack([(y - k) & 3 for k in range(YS)]).astype(jnp.int32)
    pieces.append(joined(at, quarters))
    pieces.append(last)
    cot_pieces = pieces

    masked_core = swap_core(masked)
    masked_zh = swap_zh(masked)
    masked_far = swap_core(masked_zh)

    def token_block_at(yy):
        e = (yy - x) & 3
        there = jnp.where(e == 0, SPREAD[0], jnp.where(e == 2, SPREAD[2], e))
        return (-there) & 3

    order = jnp.stack([token_block_at((y + k) & 3) for k in range(YS)]).astype(jnp.int32)

    def output_half(own, other, near):
        chunks = forward(order, hidden_pieces, own, other)
        own_chunk = chunks[0]
        got = []
        for k in (1, 2, 3):
            got.append(shift_y(chunks[k], k))
        total = own_chunk.astype(f32)
        for piece in got:
            total = total + piece.astype(f32)
        sent = total.astype(bf16)
        got = swap_zl_half(sent, near)
        total = (total + got.astype(f32)).astype(bf16)
        total = jnp.where(
            core == 0, total, jnp.concatenate([total[:, cols:], total[:, :cols]], axis=1)
        )
        return place_output(total, near)

    out_near = output_half(masked, masked_core, True)
    out_far = output_half(masked_zh, masked_far, False)
    output = jnp.where(zl == zh, out_near, out_far)

    back = backward(cot_pieces, [masked, masked_zh, masked_core, masked_far])
    got = []
    for k in (1, 2, 3):
        got.append(shift_x(back[k], -k))
    hidden_grad = back[0].astype(f32)
    for piece in got:
        hidden_grad = hidden_grad + piece.astype(f32)
    hidden_grad = hidden_grad.astype(bf16)

    away, turned = gradient_away(hidden_pieces, cot_pieces)
    stay = gradient_stay(turned, hidden_pieces, cot_pieces)
    from_core = swap_core(away)
    far = (stay[:, cols:].astype(f32) + from_core[:, cols:].astype(f32)).astype(bf16)
    from_zh = swap_zh(far)
    summed = stay[:, :cols].astype(f32) + from_core[:, :cols].astype(f32) + from_zh.astype(f32)

    moment_blocks = jnp.concatenate(
        [arranged(saved_first), arranged(saved_second)], axis=1
    )
    moments = to_columns(moment_blocks)
    moments = to_rows(moments)
    first = moments[:, :band].reshape(rows, cols).astype(f32)
    second = moments[:, band:].reshape(rows, cols).astype(f32)
    weight = weight.astype(f32)

    keep = mask.astype(f32)
    grad = keep * summed
    new_first = beta_first * first + (1.0 - beta_first) * grad
    new_second = beta_second * second + (1.0 - beta_second) * grad * grad
    corr_first = 1.0 - beta_first ** (STEP + 1)
    corr_second = 1.0 - beta_second ** (STEP + 1)
    update = new_first / corr_first / (jnp.sqrt(new_second / corr_second) + epsilon)
    new_weight = keep * (weight - learn_rate * (update + decay_rate * weight))
    return (output, hidden_grad, new_weight, new_first, new_second)


def solution(mesh):
    return jax.shard_map(
        body,
        mesh=mesh,
        in_specs=(
            P(("fsdp", "tensor"), None),
            P(("fsdp", "tensor"), None),
            P(("fsdp", "tensor"), None),
            P(("fsdp", "tensor")),
            P("tensor", "fsdp"),
            P("fsdp", "tensor"),
            P("fsdp", None),
        ),
        out_specs=(
            P("fsdp", "tensor"),
            P("fsdp", "tensor"),
            P("tensor", "fsdp"),
            P("tensor", "fsdp"),
            P("tensor", "fsdp"),
        ),
        check_vma=False,
    )
```
